32 devices in a mesh: seg: 4 (over z), slab: 8 (over y, x, core).
Axes of the slice: x: 2, y: 2, z: 4, core: 2. Of those that a mesh axis runs over, the one named last changes fastest.
Arguments:
- checkpoints: float32 [4, 32, 256, 512], P('seg', 'slab'), may hold values from 0 to 1
- control: float32 [4, 32, 256, 512], P('seg', 'slab'), may hold values from -4 to 4
- rate: float32 [32, 256, 512], P('slab'), may hold values from 0.25 to 2.5
- target: float32 [32, 256, 512], P('slab'), may hold values from 0 to 1
Outputs:
- new_checkpoints: float32 [4, 32, 256, 512], P('seg', 'slab')
- new_control: float32 [4, 32, 256, 512], P('seg', 'slab')
The draws below stay inside these ranges and needn't reach their ends.
All inputs are finite; a program needn't handle non-finite values.
Results may differ from the reference program's by a relative error of at most 0.00002.
Values sent between devices are 32-bit elements; how exact they have to be, the bound alone decides.
A program may use at most 128 MiB of HBM per device.

```python
import math
import jax
import jax.numpy as jnp

GX = 256
GY = 512
STEPS = 2
SEGS = 4
NZ = 32


def block_levels(stream_key, dims, split, low, largest):
    factor_of = 1.0
    for position, parts in split:
        steps = jax.random.uniform(jax.random.fold_in(jax.random.fold_in(stream_key, 6), position), (parts,), jnp.float32, low / len(split), largest / len(split))
        factor_of = factor_of * jnp.repeat(jnp.exp(steps), dims[position] // parts).reshape((-1,) + (1,) * (len(dims) - 1 - position))
    return factor_of


def normal_values(stream_key, dims, spread, bound, cuts=(), held_as=jnp.bfloat16):
    entries = spread * jax.random.normal(stream_key, dims, jnp.float32)
    if cuts:
        entries = entries * block_levels(stream_key, dims, cuts, -0.22, 0.18)
    return jnp.clip(entries, -bound, bound).astype(held_as)


def setup_inputs(seed: int = 0) -> dict:
    key_of = jax.random.split(jax.random.key(seed), 5)
    return {
        "checkpoints": jnp.clip(1.0 * jax.random.uniform(key_of[0], (SEGS, NZ, GX, GY), jnp.float32) ** block_levels(key_of[0], (SEGS, NZ, GX, GY), ((0, 4), (1, 8)), -0.2, 0.2), 0.0, 1.0),
        "control": normal_values(key_of[1], (SEGS, NZ, GX, GY), 0.5, 4.0, ((0, 4), (1, 8)), jnp.float32),
        "rate": jnp.clip(jnp.exp(math.log(2.5) - 2.3025851 * jax.random.uniform(key_of[2], (NZ, GX, GY), jnp.float32) ** block_levels(key_of[2], (NZ, GX, GY), ((0, 8),), -0.2, 0.2)), 0.25, 2.5),
        "target": jnp.clip(1.0 * jax.random.uniform(key_of[3], (NZ, GX, GY), jnp.float32) ** block_levels(key_of[3], (NZ, GX, GY), ((0, 8),), -0.2, 0.2), 0.0, 1.0),
    }


def laplace(field):
    padded = jnp.pad(field, 1)
    beside = padded[2:, 1:-1, 1:-1] + padded[:-2, 1:-1, 1:-1]
    beside = beside + padded[1:-1, 2:, 1:-1] + padded[1:-1, :-2, 1:-1]
    beside = beside + padded[1:-1, 1:-1, 2:] + padded[1:-1, 1:-1, :-2]
    return beside - 6.0 * field

def reference(checkpoints, control, rate, target):
    ends = []
    states = []
    for k in range(SEGS):
        state = checkpoints[k]
        path = [state]
        for t in range(STEPS):
            state = state + 0.1 * (laplace(state) + rate * state * (1.0 - state) + control[k])
            path.append(state)
        ends.append(state)
        states.append(path)
    grad_control = []
    grad_start = []
    prior = jnp.zeros_like(target)
    for k in range(SEGS):
        following = target if k == SEGS - 1 else checkpoints[k + 1]
        defect = ends[k] - following
        costate = defect
        total = jnp.zeros_like(target)
        for t in range(STEPS - 1, -1, -1):
            total = total + costate
            costate = costate + 0.1 * (laplace(costate) + rate * (1.0 - 2.0 * states[k][t]) * costate)
        grad_control.append(0.1 * total)
        grad_start.append(costate - prior)
        prior = defect
    grad_control = jnp.stack(grad_control)
    grad_start = jnp.stack(grad_start)
    squared = jnp.sum(grad_control * grad_control) + jnp.sum(grad_start * grad_start)
    count = 2.0 * SEGS * NZ * GX * GY
    scale = 0.5 / jnp.sqrt(squared / count + 1e-06)
    return (checkpoints - scale * grad_start, control - scale * grad_control)
```

```python
import functools

import jax
import jax.numpy as jnp
from jax import lax
from jax.experimental import pallas as pl
from jax.experimental.pallas import tpu as pltpu
from jax.sharding import PartitionSpec as P

CHUNKS = 8
TILE = 16
PAD = 8
LAG_U = 3
LAG_1 = 1
LAG_0 = 2
LAG_S = 3
MESH = pl.DeviceIdType.MESH


def kernel(
    n_seg, n_slab,
    cp, ctl_in, rate_in, target,
    gs_out, gc_out, tot_out,
    u0, u1, l2, l1, ctl, rat, end, cpn, prior, gs, gc, acc, slot_a, slot_b,
    sem_u0, sem_ctl, sem_rat, sem_alt_c, sem_alt_p, sem_gs, sem_gc,
    hs, hr, zs, zr, as_, ar, bs, br,
):
    me_seg = lax.axis_index("seg")
    me_slab = lax.axis_index("slab")
    layers, rows, cols = cp.shape[1:]
    size = rows // CHUNKS
    tiles = size // TILE
    top = layers + 1
    has_low = me_slab > 0
    has_high = me_slab < n_slab - 1
    first = me_seg == 0
    last = me_seg == n_seg - 1

    def span(c):
        return pl.ds(pl.multiple_of(c * size, size), size)

    def padded(c):
        return pl.ds(pl.multiple_of(c * size + PAD, 8), size)

    def load_u0(c):
        return pltpu.make_async_copy(
            cp.at[0, :, span(c)], u0.at[pl.ds(1, layers), padded(c)], sem_u0.at[c])

    def load_ctl(c):
        return pltpu.make_async_copy(ctl_in.at[0, :, span(c)], ctl.at[:, span(c)], sem_ctl.at[c])

    def load_rat(c):
        return pltpu.make_async_copy(rate_in.at[:, span(c)], rat.at[:, span(c)], sem_rat.at[c])

    def alt_c(c):
        return pltpu.make_async_copy(target.at[:, span(c)], cpn.at[:, span(c)], sem_alt_c.at[c])

    def alt_p(c):
        return pltpu.make_async_copy(cp.at[0, :, span(c)], prior.at[:, span(c)], sem_alt_p.at[c])

    def save_gs(c):
        return pltpu.make_async_copy(gs.at[:, span(c)], gs_out.at[:, span(c)], sem_gs.at[c])

    def save_gc(c):
        return pltpu.make_async_copy(gc.at[:, span(c)], gc_out.at[:, span(c)], sem_gc.at[c])

    def halo_down(k, buf, c):
        src = cp.at[0, 0, span(c)] if buf is u0 else buf.at[1, padded(c)]
        return pltpu.make_async_remote_copy(
            src, buf.at[top, padded(c)], hs.at[k, 0, c], hr.at[k, 0, c],
            device_id={"slab": me_slab - 1}, device_id_type=MESH)

    def halo_up(k, buf, c):
        src = cp.at[0, layers - 1, span(c)] if buf is u0 else buf.at[layers, padded(c)]
        return pltpu.make_async_remote_copy(
            src, buf.at[0, padded(c)], hs.at[k, 1, c], hr.at[k, 1, c],
            device_id={"slab": me_slab + 1}, device_id_type=MESH)

    def send_halo(k, buf, c):
        @pl.when(has_low)
        def _():
            halo_down(k, buf, c).start()

        @pl.when(has_high)
        def _():
            halo_up(k, buf, c).start()

    def wait_halo(k, buf, c):
        @pl.when(has_high)
        def _():
            halo_down(k, buf, c).wait_recv()

        @pl.when(has_low)
        def _():
            halo_up(k, buf, c).wait_recv()

    def send_cp(c):
        return pltpu.make_async_remote_copy(
            cp.at[0, :, span(c)], cpn.at[:, span(c)], zs.at[0, c], zr.at[0, c],
            device_id={"seg": me_seg - 1}, device_id_type=MESH)

    def send_end(c):
        return pltpu.make_async_remote_copy(
            end.at[:, span(c)], prior.at[:, span(c)], zs.at[1, c], zr.at[1, c],
            device_id={"seg": me_seg + 1}, device_id_type=MESH)

    barrier = pltpu.get_barrier_semaphore()
    for d in range(1, n_slab):
        pl.semaphore_signal(
            barrier, inc=1, device_id={"slab": lax.rem(me_slab + d, n_slab)}, device_id_type=MESH)
    for d in range(1, n_seg):
        pl.semaphore_signal(
            barrier, inc=1, device_id={"seg": lax.rem(me_seg + d, n_seg)}, device_id_type=MESH)

    @pl.loop(0, CHUNKS)
    def _(c):
        load_u0(c).start()
        load_ctl(c).start()
        load_rat(c).start()

    edge = jnp.zeros((PAD, cols), jnp.float32)
    for buf in (u0, u1, l2, l1):
        for z in range(1, top):
            buf[z, pl.ds(0, PAD), :] = edge
            buf[z, pl.ds(rows + PAD, PAD), :] = edge

    def clear(z):
        @pl.loop(0, rows // PAD)
        def _(i):
            for buf in (u0, u1, l2, l1):
                buf[z, pl.ds(pl.multiple_of(i * PAD + PAD, 8), PAD), :] = edge

    @pl.when(jnp.logical_not(has_low))
    def _():
        clear(0)

    @pl.when(jnp.logical_not(has_high))
    def _():
        clear(top)

    acc[...] = jnp.zeros_like(acc)
    pl.semaphore_wait(barrier, n_slab - 1 + n_seg - 1)

    @pl.loop(0, CHUNKS)
    def _(c):
        send_halo(0, u0, c)

        @pl.when(jnp.logical_not(first))
        def _():
            send_cp(c).start()

    @pl.loop(0, CHUNKS)
    def _(c):
        @pl.when(last)
        def _():
            alt_c(c).start()

        @pl.when(first)
        def _():
            alt_p(c).start()

    lane = lax.broadcasted_iota(jnp.int32, (TILE, cols), 1)
    at_left = lane == 0
    at_right = lane == cols - 1

    def laplace(buf, z, r):
        tall = buf[z, pl.ds(pl.multiple_of(r - PAD, 8), TILE + 2 * PAD), :]
        mid = tall[PAD:PAD + TILE]
        beside = buf[z + 1, pl.ds(r, TILE), :] + buf[z - 1, pl.ds(r, TILE), :]
        beside = beside + (tall[PAD + 1:PAD + 1 + TILE] + tall[PAD - 1:PAD - 1 + TILE])
        right = jnp.where(at_right, 0.0, pltpu.roll(mid, cols - 1, 1))
        left = jnp.where(at_left, 0.0, pltpu.roll(mid, 1, 1))
        return mid, beside + (right + left) - 6.0 * mid

    def each_tile(c, body):
        @pl.loop(0, tiles)
        def _(i):
            r = pl.multiple_of(c * size + i * TILE, 8)
            for z in range(layers):
                body(z, r, pl.ds(r, TILE), pl.multiple_of(r + PAD, 8))

    def add_square(v):
        sq = v * v
        part = sq[:PAD]
        for i in range(1, TILE // PAD):
            part = part + sq[i * PAD:(i + 1) * PAD]
        acc[...] = acc[...] + part

    def forward(src, c, dst):
        def body(z, r, at, p):
            u, lap = laplace(src, z + 1, p)
            new = u + 0.1 * (lap + rat[z, at, :] * u * (1.0 - u) + ctl[z, at, :])
            if dst is u1:
                u1[z + 1, pl.ds(p, TILE), :] = new
            else:
                end[z, at, :] = new
        each_tile(c, body)

    load_u0(0).wait()

    @pl.loop(0, CHUNKS + LAG_U)
    def _(i):
        @pl.when(i < CHUNKS)
        def _():
            @pl.when(i < CHUNKS - 1)
            def _():
                load_u0(i + 1).wait()
            load_ctl(i).wait()
            load_rat(i).wait()
            wait_halo(0, u0, i)
            forward(u0, i, u1)
            send_halo(1, u1, i)

        @pl.when(i >= LAG_U)
        def _():
            c = i - LAG_U
            wait_halo(1, u1, c)
            forward(u1, c, end)

            @pl.when(jnp.logical_not(last))
            def _():
                send_end(c).start()

    def do_defect(c):
        @pl.when(last)
        def _():
            alt_c(c).wait()

        @pl.when(jnp.logical_not(last))
        def _():
            send_cp(c).wait_recv()

        def body(z, r, at, p):
            l2[z + 1, pl.ds(p, TILE), :] = end[z, at, :] - cpn[z, at, :]
        each_tile(c, body)
        send_halo(2, l2, c)

    def do_l1(c):
        wait_halo(2, l2, c)

        def body(z, r, at, p):
            lam, lap = laplace(l2, z + 1, p)
            new = lam + 0.1 * (lap + rat[z, at, :] * (1.0 - 2.0 * u1[z + 1, pl.ds(p, TILE), :]) * lam)
            l1[z + 1, pl.ds(p, TILE), :] = new
            g = 0.1 * (lam + new)
            gc[z, at, :] = g
            add_square(g)
        each_tile(c, body)
        send_halo(3, l1, c)
        save_gc(c).start()

    def do_l0(c):
        wait_halo(3, l1, c)

        def body(z, r, at, p):
            lam, lap = laplace(l1, z + 1, p)
            start = u0[z + 1, pl.ds(p, TILE), :]
            gs[z, at, :] = lam + 0.1 * (lap + rat[z, at, :] * (1.0 - 2.0 * start) * lam)
        each_tile(c, body)

    def do_start(c):
        @pl.when(first)
        def _():
            alt_p(c).wait()

        @pl.when(jnp.logical_not(first))
        def _():
            send_end(c).wait_recv()

        def body(z, r, at, p):
            g = gs[z, at, :] - (prior[z, at, :] - u0[z + 1, pl.ds(p, TILE), :])
            gs[z, at, :] = g
            add_square(g)
        each_tile(c, body)
        save_gs(c).start()

    @pl.loop(0, CHUNKS + LAG_S)
    def _(i):
        @pl.when(i < CHUNKS)
        def _():
            do_defect(i)

        @pl.when(jnp.logical_and(i >= LAG_1, i < CHUNKS + LAG_1))
        def _():
            do_l1(i - LAG_1)

        @pl.when(jnp.logical_and(i >= LAG_0, i < CHUNKS + LAG_0))
        def _():
            do_l0(i - LAG_0)

        @pl.when(i >= LAG_S)
        def _():
            do_start(i - LAG_S)

    tile = acc[:, :128]
    for j in range(1, cols // 128):
        tile = tile + acc[:, j * 128:(j + 1) * 128]

    def total(value, slots, axis, me, count, ss, sr):
        def copy(d, owner, device):
            return pltpu.make_async_remote_copy(
                slots.at[owner], slots.at[owner], ss.at[d], sr.at[owner],
                device_id={axis: device}, device_id_type=MESH)

        slots[me] = value
        for d in range(1, count):
            copy(d, me, lax.rem(me + d, count)).start()
        for d in range(1, count):
            source = lax.rem(me + count - d, count)
            copy(d, source, source).wait_recv()
        result = slots[0]
        for j in range(1, count):
            result = result + slots[j]
        for d in range(1, count):
            copy(d, me, lax.rem(me + d, count)).wait_send()
        return result

    tile = total(tile, slot_a, "slab", me_slab, n_slab, as_, ar)
    tile = total(tile, slot_b, "seg", me_seg, n_seg, bs, br)
    tot_out[...] = tile

    @pl.loop(0, CHUNKS)
    def _(c):
        save_gs(c).wait()
        save_gc(c).wait()
        for k, buf in enumerate((u0, u1, l2, l1)):
            @pl.when(has_low)
            def _():
                halo_down(k, buf, c).wait_send()

            @pl.when(has_high)
            def _():
                halo_up(k, buf, c).wait_send()

        @pl.when(jnp.logical_not(first))
        def _():
            send_cp(c).wait_send()

        @pl.when(jnp.logical_not(last))
        def _():
            send_end(c).wait_send()


def per_device(checkpoints, control, rate, target):
    n_seg = lax.axis_size("seg")
    n_slab = lax.axis_size("slab")
    layers, rows, cols = rate.shape
    f32 = jnp.float32
    block = pltpu.VMEM((layers, rows, cols), f32)
    wide = pltpu.VMEM((layers + 2, rows + 2 * PAD, cols), f32)
    dma = pltpu.SemaphoreType.DMA
    anywhere = pl.BlockSpec(memory_space=pl.ANY)
    gs, gc, tot = pl.pallas_call(
        functools.partial(kernel, n_seg, n_slab),
        out_shape=(
            jax.ShapeDtypeStruct((layers, rows, cols), f32),
            jax.ShapeDtypeStruct((layers, rows, cols), f32),
            jax.ShapeDtypeStruct((8, 128), f32),
        ),
        in_specs=[anywhere] * 4,
        out_specs=(anywhere, anywhere, pl.BlockSpec(memory_space=pltpu.VMEM)),
        scratch_shapes=[
            wide, wide, wide, wide,
            block, block, block, block, block, block, block,
            pltpu.VMEM((PAD, cols), f32),
            pltpu.VMEM((n_slab, 8, 128), f32),
            pltpu.VMEM((n_seg, 8, 128), f32),
            dma((CHUNKS,)), dma((CHUNKS,)), dma((CHUNKS,)),
            dma((CHUNKS,)), dma((CHUNKS,)), dma((CHUNKS,)), dma((CHUNKS,)),
            dma((4, 2, CHUNKS)), dma((4, 2, CHUNKS)),
            dma((2, CHUNKS)), dma((2, CHUNKS)),
            dma((n_slab,)), dma((n_slab,)),
            dma((n_seg,)), dma((n_seg,)),
        ],
        compiler_params=pltpu.CompilerParams(
            collective_id=0, has_side_effects=True, vmem_limit_bytes=58 << 20
        ),
        name="shooting",
    )(checkpoints, control, rate, target)
    count = 2.0 * n_seg * n_slab * rate.size
    scale = 0.5 / jnp.sqrt(jnp.sum(tot) / count + 1e-06)
    return checkpoints - scale * gs[None], control - scale * gc[None]


def solution(mesh):
    return jax.shard_map(
        per_device,
        mesh=mesh,
        in_specs=(
            P("seg", "slab", None, None),
            P("seg", "slab", None, None),
            P("slab", None, None),
            P("slab", None, None),
        ),
        out_specs=(P("seg", "slab", None, None), P("seg", "slab", None, None)),
        check_vma=False,
    )
```

```python
import functools

import jax
import jax.numpy as jnp
from jax import lax
from jax.experimental import pallas as pl
from jax.experimental.pallas import tpu as pltpu
from jax.sharding import PartitionSpec as P

CHUNKS = 8
PARTS = 8
TILE = 16
PAD = 8
LAG_U = 2
AHEAD = 3
LAG_1 = 1
LAG_0 = 2
LAG_S = 3
MESH = pl.DeviceIdType.MESH


def kernel(
    n_seg, n_slab,
    cp, ctl_in, rate_in, target,
    u0, ctl, gs, gc, tot_out,
    u1, l2, l1, rat, end, cpn, prior, acc, slot_a, slot_b,
    sem_u0, sem_ctl, sem_rat, sem_alt_c, sem_alt_p,
    hs, hr, zs, zr, as_, ar, bs, br,
):
    me_seg = lax.axis_index("seg")
    me_slab = lax.axis_index("slab")
    layers, rows, cols = cp.shape[1:]
    size = rows // CHUNKS
    tiles = size // TILE
    top = layers + 1
    has_low = me_slab > 0
    has_high = me_slab < n_slab - 1
    first = me_seg == 0
    last = me_seg == n_seg - 1

    def span(c):
        return pl.ds(pl.multiple_of(c * size, size), size)

    def padded(c):
        return pl.ds(pl.multiple_of(c * size + PAD, 8), size)

    def load_u0(c):
        return pltpu.make_async_copy(
            cp.at[0, :, span(c)], u0.at[pl.ds(1, layers), padded(c)], sem_u0.at[c])

    def load_ctl(c):
        return pltpu.make_async_copy(ctl_in.at[0, :, span(c)], ctl.at[:, span(c)], sem_ctl.at[c])

    def load_rat(c):
        return pltpu.make_async_copy(rate_in.at[:, span(c)], rat.at[:, span(c)], sem_rat.at[c])

    def alt_c(c):
        return pltpu.make_async_copy(target.at[:, span(c)], cpn.at[:, span(c)], sem_alt_c.at[c])

    def alt_p(c):
        return pltpu.make_async_copy(cp.at[0, :, span(c)], prior.at[:, span(c)], sem_alt_p.at[c])

    def halo_down(k, buf, c):
        src = cp.at[0, 0, span(c)] if buf is u0 else buf.at[1, padded(c)]
        return pltpu.make_async_remote_copy(
            src, buf.at[top, padded(c)], hs.at[k, 0, c], hr.at[k, 0, c],
            device_id={"slab": me_slab - 1}, device_id_type=MESH)

    def halo_up(k, buf, c):
        src = cp.at[0, layers - 1, span(c)] if buf is u0 else buf.at[layers, padded(c)]
        return pltpu.make_async_remote_copy(
            src, buf.at[0, padded(c)], hs.at[k, 1, c], hr.at[k, 1, c],
            device_id={"slab": me_slab + 1}, device_id_type=MESH)

    def send_halo(k, buf, c):
        @pl.when(has_low)
        def _():
            halo_down(k, buf, c).start()

        @pl.when(has_high)
        def _():
            halo_up(k, buf, c).start()

    def wait_halo(k, buf, c):
        @pl.when(has_high)
        def _():
            halo_down(k, buf, c).wait_recv()

        @pl.when(has_low)
        def _():
            halo_up(k, buf, c).wait_recv()

    def send_cp(c):
        return pltpu.make_async_remote_copy(
            cp.at[0, :, span(c)], cpn.at[:, span(c)], zs.at[0, c], zr.at[0, c],
            device_id={"seg": me_seg - 1}, device_id_type=MESH)

    def send_end(c):
        return pltpu.make_async_remote_copy(
            end.at[:, span(c)], prior.at[:, span(c)], zs.at[1, c], zr.at[1, c],
            device_id={"seg": me_seg + 1}, device_id_type=MESH)

    barrier = pltpu.get_barrier_semaphore()
    for d in range(1, n_slab):
        pl.semaphore_signal(
            barrier, inc=1, device_id={"slab": lax.rem(me_slab + d, n_slab)}, device_id_type=MESH)
    for d in range(1, n_seg):
        pl.semaphore_signal(
            barrier, inc=1, device_id={"seg": lax.rem(me_seg + d, n_seg)}, device_id_type=MESH)

    @pl.loop(0, CHUNKS)
    def _(c):
        load_u0(c).start()
        load_ctl(c).start()
        load_rat(c).start()

    edge = jnp.zeros((PAD, cols), jnp.float32)
    for buf in (u0, u1, l2, l1):
        for z in range(1, top):
            buf[z, pl.ds(0, PAD), :] = edge
            buf[z, pl.ds(rows + PAD, PAD), :] = edge

    def clear(z):
        @pl.loop(0, rows // PAD)
        def _(i):
            for buf in (u0, u1, l2, l1):
                buf[z, pl.ds(pl.multiple_of(i * PAD + PAD, 8), PAD), :] = edge

    @pl.when(jnp.logical_not(has_low))
    def _():
        clear(0)

    @pl.when(jnp.logical_not(has_high))
    def _():
        clear(top)

    acc[...] = jnp.zeros_like(acc)
    pl.semaphore_wait(barrier, n_slab - 1 + n_seg - 1)

    for c in range(AHEAD):
        send_halo(0, u0, c)

    @pl.loop(0, CHUNKS)
    def _(c):
        @pl.when(jnp.logical_not(first))
        def _():
            send_cp(c).start()

    @pl.loop(0, CHUNKS)
    def _(c):
        @pl.when(last)
        def _():
            alt_c(c).start()

        @pl.when(first)
        def _():
            alt_p(c).start()

    lane = lax.broadcasted_iota(jnp.int32, (TILE, cols), 1)
    at_left = lane == 0
    at_right = lane == cols - 1

    def laplace(buf, z, r):
        tall = buf[z, pl.ds(pl.multiple_of(r - PAD, 8), TILE + 2 * PAD), :]
        mid = tall[PAD:PAD + TILE]
        beside = buf[z + 1, pl.ds(r, TILE), :] + buf[z - 1, pl.ds(r, TILE), :]
        beside = beside + (tall[PAD + 1:PAD + 1 + TILE] + tall[PAD - 1:PAD - 1 + TILE])
        right = jnp.where(at_right, 0.0, pltpu.roll(mid, cols - 1, 1))
        left = jnp.where(at_left, 0.0, pltpu.roll(mid, 1, 1))
        return mid, beside + (right + left) - 6.0 * mid

    def each_tile(c, body):
        @pl.loop(0, tiles)
        def _(i):
            r = pl.multiple_of(c * size + i * TILE, 8)
            for z in range(layers):
                body(z, r, pl.ds(r, TILE), pl.multiple_of(r + PAD, 8))

    def add_square(v):
        sq = v * v
        part = sq[:PAD]
        for i in range(1, TILE // PAD):
            part = part + sq[i * PAD:(i + 1) * PAD]
        acc[...] = acc[...] + part

    def forward(src, c, dst):
        def body(z, r, at, p):
            u, lap = laplace(src, z + 1, p)
            new = u + 0.1 * (lap + rat[z, at, :] * u * (1.0 - u) + ctl[z, at, :])
            if dst is u1:
                u1[z + 1, pl.ds(p, TILE), :] = new
            else:
                end[z, at, :] = new
        each_tile(c, body)

    load_u0(0).wait()

    @pl.loop(0, CHUNKS + LAG_U)
    def _(i):
        @pl.when(i < CHUNKS)
        def _():
            @pl.when(i < CHUNKS - 1)
            def _():
                load_u0(i + 1).wait()
            load_ctl(i).wait()
            load_rat(i).wait()

            @pl.when(i < CHUNKS - AHEAD)
            def _():
                send_halo(0, u0, i + AHEAD)
            wait_halo(0, u0, i)
            forward(u0, i, u1)
            send_halo(1, u1, i)

        @pl.when(i >= LAG_U)
        def _():
            c = i - LAG_U
            wait_halo(1, u1, c)
            forward(u1, c, end)

            @pl.when(jnp.logical_not(last))
            def _():
                send_end(c).start()

    def do_defect(c):
        @pl.when(last)
        def _():
            alt_c(c).wait()

        @pl.when(jnp.logical_not(last))
        def _():
            send_cp(c).wait_recv()

        def body(z, r, at, p):
            l2[z + 1, pl.ds(p, TILE), :] = end[z, at, :] - cpn[z, at, :]
        each_tile(c, body)
        send_halo(2, l2, c)

    def do_l1(c):
        wait_halo(2, l2, c)

        def body(z, r, at, p):
            lam, lap = laplace(l2, z + 1, p)
            new = lam + 0.1 * (lap + rat[z, at, :] * (1.0 - 2.0 * u1[z + 1, pl.ds(p, TILE), :]) * lam)
            l1[z + 1, pl.ds(p, TILE), :] = new
            g = 0.1 * (lam + new)
            gc[z, at, :] = g
            add_square(g)
        each_tile(c, body)
        send_halo(3, l1, c)

    def do_l0(c):
        wait_halo(3, l1, c)

        def body(z, r, at, p):
            lam, lap = laplace(l1, z + 1, p)
            start = u0[z + 1, pl.ds(p, TILE), :]
            gs[z, at, :] = lam + 0.1 * (lap + rat[z, at, :] * (1.0 - 2.0 * start) * lam)
        each_tile(c, body)

    def do_start(c):
        @pl.when(first)
        def _():
            alt_p(c).wait()

        @pl.when(jnp.logical_not(first))
        def _():
            send_end(c).wait_recv()

        def body(z, r, at, p):
            g = gs[z, at, :] - (prior[z, at, :] - u0[z + 1, pl.ds(p, TILE), :])
            gs[z, at, :] = g
            add_square(g)
        each_tile(c, body)

    @pl.loop(0, CHUNKS + LAG_S)
    def _(i):
        @pl.when(i < CHUNKS)
        def _():
            do_defect(i)

        @pl.when(jnp.logical_and(i >= LAG_1, i < CHUNKS + LAG_1))
        def _():
            do_l1(i - LAG_1)

        @pl.when(jnp.logical_and(i >= LAG_0, i < CHUNKS + LAG_0))
        def _():
            do_l0(i - LAG_0)

        @pl.when(i >= LAG_S)
        def _():
            do_start(i - LAG_S)

    tile = acc[:, :128]
    for j in range(1, cols // 128):
        tile = tile + acc[:, j * 128:(j + 1) * 128]

    def total(value, slots, axis, me, count, ss, sr):
        def copy(d, owner, device):
            return pltpu.make_async_remote_copy(
                slots.at[owner], slots.at[owner], ss.at[d], sr.at[owner],
                device_id={axis: device}, device_id_type=MESH)

        slots[me] = value
        for d in range(1, count):
            copy(d, me, lax.rem(me + d, count)).start()
        for d in range(1, count):
            source = lax.rem(me + count - d, count)
            copy(d, source, source).wait_recv()
        result = slots[0]
        for j in range(1, count):
            result = result + slots[j]
        sent.extend(copy(d, me, lax.rem(me + d, count)) for d in range(1, count))
        return result

    sent = []
    tile = total(tile, slot_a, "slab", me_slab, n_slab, as_, ar)
    tile = total(tile, slot_b, "seg", me_seg, n_seg, bs, br)
    tot_out[...] = tile
    for copy in sent:
        copy.wait_send()

    @pl.loop(0, CHUNKS)
    def _(c):
        for k, buf in enumerate((u0, u1, l2, l1)):
            @pl.when(has_low)
            def _():
                halo_down(k, buf, c).wait_send()

            @pl.when(has_high)
            def _():
                halo_up(k, buf, c).wait_send()

        @pl.when(jnp.logical_not(first))
        def _():
            send_cp(c).wait_send()

        @pl.when(jnp.logical_not(last))
        def _():
            send_end(c).wait_send()


def update_kernel(
    count, u0, ctl, gs, gc, tot, new_cp, new_ctl, out_a, out_b, sem_a, sem_b
):
    layers, rows, cols = ctl.shape
    size = rows // PARTS
    sum_of = jnp.sum(jnp.sum(tot[...], axis=0, keepdims=True), axis=1, keepdims=True)
    scale = jnp.broadcast_to(0.5 / jnp.sqrt(sum_of / count + 1e-06), (PAD, cols))

    def save(c):
        at = pl.ds(pl.multiple_of(c * size, size), size)
        return (
            pltpu.make_async_copy(out_a.at[:, at], new_cp.at[0, :, at], sem_a.at[c]),
            pltpu.make_async_copy(out_b.at[:, at], new_ctl.at[0, :, at], sem_b.at[c]),
        )

    @pl.loop(0, PARTS)
    def _(c):
        @pl.loop(0, size // PAD)
        def _(i):
            r = pl.multiple_of(c * size + i * PAD, 8)
            at = pl.ds(r, PAD)
            for z in range(layers):
                start = u0[z + 1, pl.ds(pl.multiple_of(r + PAD, 8), PAD), :]
                out_a[z, at, :] = start - scale * gs[z, at, :]
                out_b[z, at, :] = ctl[z, at, :] - scale * gc[z, at, :]
        for copy in save(c):
            copy.start()

    @pl.loop(0, PARTS)
    def _(c):
        for copy in save(c):
            copy.wait()


def per_device(checkpoints, control, rate, target):
    n_seg = lax.axis_size("seg")
    n_slab = lax.axis_size("slab")
    layers, rows, cols = rate.shape
    f32 = jnp.float32
    block = pltpu.VMEM((layers, rows, cols), f32)
    wide = pltpu.VMEM((layers + 2, rows + 2 * PAD, cols), f32)
    dma = pltpu.SemaphoreType.DMA
    hbm = pl.BlockSpec(memory_space=pltpu.HBM)
    vmem = pl.BlockSpec(memory_space=pltpu.VMEM)
    kept = pl.pallas_call(
        functools.partial(kernel, n_seg, n_slab),
        out_shape=(wide, block, block, block, pltpu.VMEM((8, 128), f32)),
        in_specs=[hbm] * 4,
        out_specs=(vmem,) * 5,
        scratch_shapes=[
            wide, wide, wide,
            block, block, block, block,
            pltpu.VMEM((PAD, cols), f32),
            pltpu.VMEM((n_slab, 8, 128), f32),
            pltpu.VMEM((n_seg, 8, 128), f32),
            dma((CHUNKS,)), dma((CHUNKS,)), dma((CHUNKS,)),
            dma((CHUNKS,)), dma((CHUNKS,)),
            dma((4, 2, CHUNKS)), dma((4, 2, CHUNKS)),
            dma((2, CHUNKS)), dma((2, CHUNKS)),
            dma((n_slab,)), dma((n_slab,)),
            dma((n_seg,)), dma((n_seg,)),
        ],
        compiler_params=pltpu.CompilerParams(
            collective_id=0, has_side_effects=True, vmem_limit_bytes=50 << 20
        ),
        name="shooting",
    )(checkpoints, control, rate, target)
    count = 2.0 * n_seg * n_slab * rate.size
    return pl.pallas_call(
        functools.partial(update_kernel, count),
        out_shape=(
            jax.ShapeDtypeStruct(checkpoints.shape, f32),
            jax.ShapeDtypeStruct(control.shape, f32),
        ),
        in_specs=[vmem] * 5,
        out_specs=(hbm, hbm),
        scratch_shapes=[block, block, dma((PARTS,)), dma((PARTS,))],
        compiler_params=pltpu.CompilerParams(vmem_limit_bytes=8 << 20),
        name="update",
    )(*kept)


def solution(mesh):
    return jax.shard_map(
        per_device,
        mesh=mesh,
        in_specs=(
            P("seg", "slab", None, None),
            P("seg", "slab", None, None),
            P("slab", None, None),
            P("slab", None, None),
        ),
        out_specs=(P("seg", "slab", None, None), P("seg", "slab", None, None)),
        check_vma=False,
    )
```

```python
import functools

import jax
import jax.numpy as jnp
from jax import lax
from jax.experimental import pallas as pl
from jax.experimental.pallas import tpu as pltpu
from jax.sharding import PartitionSpec as P

CHUNKS = 8
PARTS = 8
TILE = 16
PAD = 8
LAG_U = 2
AHEAD = 3
LAG_0 = 2
LAG_S = 3
MESH = pl.DeviceIdType.MESH


def kernel(
    n_seg, n_slab,
    cp, ctl_in, rate_in, target,
    u0, ctl, gs, gc, tot_out,
    u1, l2, l1, rat, end, cpn, prior, acc, slot_a, slot_b,
    sem_u0, sem_ctl, sem_rat, sem_alt_c, sem_alt_p,
    hs, hr, zs, zr, as_, ar, bs, br,
):
    me_seg = lax.axis_index("seg")
    me_slab = lax.axis_index("slab")
    layers, rows, cols = cp.shape[1:]
    size = rows // CHUNKS
    tiles = size // TILE
    top = layers + 1
    has_low = me_slab > 0
    has_high = me_slab < n_slab - 1
    first = me_seg == 0
    last = me_seg == n_seg - 1

    def span(c):
        return pl.ds(pl.multiple_of(c * size, size), size)

    def padded(c):
        return pl.ds(pl.multiple_of(c * size + PAD, 8), size)

    def load_u0(c):
        return pltpu.make_async_copy(
            cp.at[0, :, span(c)], u0.at[pl.ds(1, layers), padded(c)], sem_u0.at[c])

    def load_ctl(c):
        return pltpu.make_async_copy(ctl_in.at[0, :, span(c)], ctl.at[:, span(c)], sem_ctl.at[c])

    def load_rat(c):
        return pltpu.make_async_copy(rate_in.at[:, span(c)], rat.at[:, span(c)], sem_rat.at[c])

    def alt_c(c):
        return pltpu.make_async_copy(target.at[:, span(c)], cpn.at[:, span(c)], sem_alt_c.at[c])

    def alt_p(c):
        return pltpu.make_async_copy(cp.at[0, :, span(c)], prior.at[:, span(c)], sem_alt_p.at[c])

    def halo_down(k, buf, c):
        src = cp.at[0, 0, span(c)] if buf is u0 else buf.at[1, padded(c)]
        return pltpu.make_async_remote_copy(
            src, buf.at[top, padded(c)], hs.at[k, 0, c], hr.at[k, 0, c],
            device_id={"slab": me_slab - 1}, device_id_type=MESH)

    def halo_up(k, buf, c):
        src = cp.at[0, layers - 1, span(c)] if buf is u0 else buf.at[layers, padded(c)]
        return pltpu.make_async_remote_copy(
            src, buf.at[0, padded(c)], hs.at[k, 1, c], hr.at[k, 1, c],
            device_id={"slab": me_slab + 1}, device_id_type=MESH)

    def send_halo(k, buf, c):
        @pl.when(has_low)
        def _():
            halo_down(k, buf, c).start()

        @pl.when(has_high)
        def _():
            halo_up(k, buf, c).start()

    def wait_halo(k, buf, c):
        @pl.when(has_high)
        def _():
            halo_down(k, buf, c).wait_recv()

        @pl.when(has_low)
        def _():
            halo_up(k, buf, c).wait_recv()

    inner = range(1, layers - 1)
    rim = (0, layers - 1)
    parts = (pl.ds(1, layers - 2), 0, layers - 1)

    def send_cp(c, part):
        at = parts[part]
        return pltpu.make_async_remote_copy(
            cp.at[0, at, span(c)], cpn.at[at, span(c)], zs.at[part + 3, c], zr.at[part + 3, c],
            device_id={"seg": me_seg - 1}, device_id_type=MESH)

    def send_end(c, part):
        at = parts[part]
        return pltpu.make_async_remote_copy(
            end.at[at, span(c)], prior.at[at, span(c)], zs.at[part, c], zr.at[part, c],
            device_id={"seg": me_seg + 1}, device_id_type=MESH)

    barrier = pltpu.get_barrier_semaphore()
    slab_peers = [{"slab": lax.rem(me_slab + d, n_slab)} for d in range(1, n_slab)]
    seg_peers = [{"seg": lax.rem(me_seg + d, n_seg)} for d in range(1, n_seg)]
    both = [
        {"seg": lax.rem(me_seg + e, n_seg), "slab": lax.rem(me_slab + d, n_slab)}
        for e in range(1, n_seg) for d in range(1, n_slab)
    ]
    direct = n_seg * n_slab <= 32
    peers = slab_peers + seg_peers + (both if direct else [])
    for peer in peers:
        pl.semaphore_signal(barrier, inc=1, device_id=peer, device_id_type=MESH)

    @pl.loop(0, CHUNKS)
    def _(c):
        load_u0(c).start()
        load_ctl(c).start()
        load_rat(c).start()

    edge = jnp.zeros((PAD, cols), jnp.float32)
    for buf in (u0, u1, l2, l1):
        for z in range(1, top):
            buf[z, pl.ds(0, PAD), :] = edge
            buf[z, pl.ds(rows + PAD, PAD), :] = edge

    def clear(z):
        @pl.loop(0, rows // PAD)
        def _(i):
            for buf in (u0, u1, l2, l1):
                buf[z, pl.ds(pl.multiple_of(i * PAD + PAD, 8), PAD), :] = edge

    @pl.when(jnp.logical_not(has_low))
    def _():
        clear(0)

    @pl.when(jnp.logical_not(has_high))
    def _():
        clear(top)

    acc[...] = jnp.zeros_like(acc)
    pl.semaphore_wait(barrier, len(peers))

    for c in range(AHEAD):
        send_halo(0, u0, c)

    @pl.when(jnp.logical_not(first))
    def _():
        @pl.loop(0, CHUNKS)
        def _(c):
            send_cp(c, 1).start()
            send_cp(c, 2).start()

        @pl.loop(0, CHUNKS)
        def _(c):
            send_cp(c, 0).start()

    @pl.loop(0, CHUNKS)
    def _(c):
        @pl.when(last)
        def _():
            alt_c(c).start()

        @pl.when(first)
        def _():
            alt_p(c).start()

    lane = lax.broadcasted_iota(jnp.int32, (TILE, cols), 1)
    at_left = lane == 0
    at_right = lane == cols - 1

    def laplace(buf, z, r):
        tall = buf[z, pl.ds(pl.multiple_of(r - PAD, 8), TILE + 2 * PAD), :]
        mid = tall[PAD:PAD + TILE]
        beside = buf[z + 1, pl.ds(r, TILE), :] + buf[z - 1, pl.ds(r, TILE), :]
        beside = beside + (tall[PAD + 1:PAD + 1 + TILE] + tall[PAD - 1:PAD - 1 + TILE])
        right = jnp.where(at_right, 0.0, pltpu.roll(mid, cols - 1, 1))
        left = jnp.where(at_left, 0.0, pltpu.roll(mid, 1, 1))
        return mid, beside + (right + left) - 6.0 * mid

    def each_tile(c, body, zs=range(layers)):
        @pl.loop(0, tiles)
        def _(i):
            r = pl.multiple_of(c * size + i * TILE, 8)
            for z in zs:
                body(z, r, pl.ds(r, TILE), pl.multiple_of(r + PAD, 8))

    def add_square(v):
        sq = v * v
        part = sq[:PAD]
        for i in range(1, TILE // PAD):
            part = part + sq[i * PAD:(i + 1) * PAD]
        acc[...] = acc[...] + part

    def forward(src, c, dst, zs):
        def body(z, r, at, p):
            u, lap = laplace(src, z + 1, p)
            new = u + 0.1 * (lap + rat[z, at, :] * u * (1.0 - u) + ctl[z, at, :])
            if dst is u1:
                u1[z + 1, pl.ds(p, TILE), :] = new
            else:
                end[z, at, :] = new
        each_tile(c, body, zs)

    load_u0(0).wait()

    @pl.loop(0, CHUNKS + LAG_U)
    def _(i):
        @pl.when(i < CHUNKS)
        def _():
            @pl.when(i < CHUNKS - 1)
            def _():
                load_u0(i + 1).wait()
            load_ctl(i).wait()
            load_rat(i).wait()

            @pl.when(i < CHUNKS - AHEAD)
            def _():
                send_halo(0, u0, i + AHEAD)
            wait_halo(0, u0, i)
            forward(u0, i, u1, range(layers))
            send_halo(1, u1, i)

        @pl.when(jnp.logical_and(i >= 1, i <= CHUNKS))
        def _():
            c = i - 1
            forward(u1, c, end, inner)

            @pl.when(jnp.logical_not(last))
            def _():
                send_end(c, 0).start()

        @pl.when(i >= LAG_U)
        def _():
            c = i - LAG_U
            wait_halo(1, u1, c)
            forward(u1, c, end, rim)

            @pl.when(jnp.logical_not(last))
            def _():
                send_end(c, 1).start()
                send_end(c, 2).start()

    def defect(c, zs):
        def body(z, r, at, p):
            l2[z + 1, pl.ds(p, TILE), :] = end[z, at, :] - cpn[z, at, :]
        each_tile(c, body, zs)

    @pl.loop(0, CHUNKS)
    def _(c):
        @pl.when(last)
        def _():
            alt_c(c).wait()

        @pl.when(jnp.logical_not(last))
        def _():
            send_cp(c, 1).wait_recv()
            send_cp(c, 2).wait_recv()
        defect(c, rim)
        send_halo(2, l2, c)

    def do_defect(c):
        @pl.when(jnp.logical_not(last))
        def _():
            send_cp(c, 0).wait_recv()
        defect(c, inner)

    def do_l1(c):
        wait_halo(2, l2, c)

        def body(z, r, at, p):
            lam, lap = laplace(l2, z + 1, p)
            new = lam + 0.1 * (lap + rat[z, at, :] * (1.0 - 2.0 * u1[z + 1, pl.ds(p, TILE), :]) * lam)
            l1[z + 1, pl.ds(p, TILE), :] = new
            g = 0.1 * (lam + new)
            gc[z, at, :] = g
            add_square(g)
        each_tile(c, body)
        send_halo(3, l1, c)

    def do_l0(c):
        wait_halo(3, l1, c)

        def body(z, r, at, p):
            lam, lap = laplace(l1, z + 1, p)
            start = u0[z + 1, pl.ds(p, TILE), :]
            gs[z, at, :] = lam + 0.1 * (lap + rat[z, at, :] * (1.0 - 2.0 * start) * lam)
        each_tile(c, body)

    def do_start(c):
        @pl.when(first)
        def _():
            alt_p(c).wait()

        @pl.when(jnp.logical_not(first))
        def _():
            for part in range(3):
                send_end(c, part).wait_recv()

        def body(z, r, at, p):
            g = gs[z, at, :] - (prior[z, at, :] - u0[z + 1, pl.ds(p, TILE), :])
            gs[z, at, :] = g
            add_square(g)
        each_tile(c, body)

    @pl.loop(0, CHUNKS + LAG_S)
    def _(i):
        @pl.when(i < CHUNKS)
        def _():
            do_defect(i)

        @pl.when(jnp.logical_and(i >= 1, i < CHUNKS))
        def _():
            do_l1(i - 1)

        @pl.when(i == CHUNKS - 1)
        def _():
            do_l1(i)

        @pl.when(jnp.logical_and(i >= LAG_0, i < CHUNKS + LAG_0))
        def _():
            do_l0(i - LAG_0)

        @pl.when(i >= LAG_S)
        def _():
            do_start(i - LAG_S)

    tile = acc[:, :128]
    for j in range(1, cols // 128):
        tile = tile + acc[:, j * 128:(j + 1) * 128]

    def total(value, slots, owner, peers, ss, sr):
        count = len(peers)

        def copy(at, peer):
            return pltpu.make_async_remote_copy(
                slots.at[at], slots.at[at], ss, sr, device_id=peer, device_id_type=MESH)

        slots[owner] = value
        for peer in peers:
            copy(owner, peer).start()
        everything = copy(pl.ds(0, count), peers[0])
        everything.wait_recv()
        result = slots[0]
        for j in range(1, count + 1):
            result = result + slots[j]
        return result, everything

    if direct:
        tile, sent_a = total(tile, slot_a, me_seg * n_slab + me_slab, peers, as_, ar)
        sent = [sent_a]
    else:
        tile, sent_a = total(tile, slot_a, me_slab, slab_peers, as_, ar)
        tile, sent_b = total(tile, slot_b, me_seg, seg_peers, bs, br)
        sent = [sent_a, sent_b]
    tot_out[...] = tile
    for copies in sent:
        copies.wait_send()

    @pl.loop(0, CHUNKS)
    def _(c):
        for k, buf in enumerate((u0, u1, l2, l1)):
            @pl.when(has_low)
            def _():
                halo_down(k, buf, c).wait_send()

            @pl.when(has_high)
            def _():
                halo_up(k, buf, c).wait_send()

        @pl.when(jnp.logical_not(first))
        def _():
            for part in range(3):
                send_cp(c, part).wait_send()

        @pl.when(jnp.logical_not(last))
        def _():
            for part in range(3):
                send_end(c, part).wait_send()


def update_kernel(
    count, u0, ctl, gs, gc, tot, new_cp, new_ctl, out_a, out_b, sem_a, sem_b
):
    layers, rows, cols = ctl.shape
    size = rows // PARTS
    sum_of = jnp.sum(jnp.sum(tot[...], axis=0, keepdims=True), axis=1, keepdims=True)
    scale = jnp.broadcast_to(0.5 / jnp.sqrt(sum_of / count + 1e-06), (PAD, cols))

    def save(c):
        at = pl.ds(pl.multiple_of(c * size, size), size)
        return (
            pltpu.make_async_copy(out_a.at[:, at], new_cp.at[0, :, at], sem_a.at[c]),
            pltpu.make_async_copy(out_b.at[:, at], new_ctl.at[0, :, at], sem_b.at[c]),
        )

    @pl.loop(0, PARTS)
    def _(c):
        @pl.loop(0, size // PAD)
        def _(i):
            r = pl.multiple_of(c * size + i * PAD, 8)
            at = pl.ds(r, PAD)
            for z in range(layers):
                start = u0[z + 1, pl.ds(pl.multiple_of(r + PAD, 8), PAD), :]
                out_a[z, at, :] = start - scale * gs[z, at, :]
                out_b[z, at, :] = ctl[z, at, :] - scale * gc[z, at, :]
        for copy in save(c):
            copy.start()

    @pl.loop(0, PARTS)
    def _(c):
        for copy in save(c):
            copy.wait()


def per_device(checkpoints, control, rate, target):
    n_seg = lax.axis_size("seg")
    n_slab = lax.axis_size("slab")
    layers, rows, cols = rate.shape
    f32 = jnp.float32
    block = pltpu.VMEM((layers, rows, cols), f32)
    wide = pltpu.VMEM((layers + 2, rows + 2 * PAD, cols), f32)
    dma = pltpu.SemaphoreType.DMA
    hbm = pl.BlockSpec(memory_space=pltpu.HBM)
    vmem = pl.BlockSpec(memory_space=pltpu.VMEM)
    kept = pl.pallas_call(
        functools.partial(kernel, n_seg, n_slab),
        out_shape=(wide, block, block, block, pltpu.VMEM((8, 128), f32)),
        in_specs=[hbm] * 4,
        out_specs=(vmem,) * 5,
        scratch_shapes=[
            wide, wide, wide,
            block, block, block, block,
            pltpu.VMEM((PAD, cols), f32),
            pltpu.VMEM((n_slab * n_seg, 8, 128), f32),
            pltpu.VMEM((n_seg, 8, 128), f32),
            dma((CHUNKS,)), dma((CHUNKS,)), dma((CHUNKS,)),
            dma((CHUNKS,)), dma((CHUNKS,)),
            dma((4, 2, CHUNKS)), dma((4, 2, CHUNKS)),
            dma((6, CHUNKS)), dma((6, CHUNKS)),
            dma(()), dma(()), dma(()), dma(()),
        ],
        compiler_params=pltpu.CompilerParams(
            collective_id=0, has_side_effects=True, vmem_limit_bytes=50 << 20
        ),
        name="shooting",
    )(checkpoints, control, rate, target)
    count = 2.0 * n_seg * n_slab * rate.size
    return pl.pallas_call(
        functools.partial(update_kernel, count),
        out_shape=(
            jax.ShapeDtypeStruct(checkpoints.shape, f32),
            jax.ShapeDtypeStruct(control.shape, f32),
        ),
        in_specs=[vmem] * 5,
        out_specs=(hbm, hbm),
        scratch_shapes=[block, block, dma((PARTS,)), dma((PARTS,))],
        compiler_params=pltpu.CompilerParams(vmem_limit_bytes=8 << 20),
        name="update",
    )(*kept)


def solution(mesh):
    return jax.shard_map(
        per_device,
        mesh=mesh,
        in_specs=(
            P("seg", "slab", None, None),
            P("seg", "slab", None, None),
            P("slab", None, None),
            P("slab", None, None),
        ),
        out_specs=(P("seg", "slab", None, None), P("seg", "slab", None, None)),
        check_vma=False,
    )
```

```python
import functools

import jax
import jax.numpy as jnp
from jax import lax
from jax.experimental import pallas as pl
from jax.experimental.pallas import tpu as pltpu
from jax.sharding import PartitionSpec as P

CHUNKS = 8
PARTS = 8
TILE = 16
PAD = 8
LAG_U = 4
AHEAD = 8
LAG_0 = 2
LAG_S = 3
MESH = pl.DeviceIdType.MESH


def kernel(
    n_seg, n_slab,
    cp, ctl_in, rate_in, target,
    u0, ctl, gs, gc, tot_out,
    u1, l2, l1, rat, end, cpn, prior, acc, slot_a, slot_b,
    sem_u0, sem_ctl, sem_rat, sem_alt_c, sem_alt_p,
    hs, hr, zs, zr, as_, ar, bs, br,
):
    me_seg = lax.axis_index("seg")
    me_slab = lax.axis_index("slab")
    layers, rows, cols = cp.shape[1:]
    size = rows // CHUNKS
    tiles = size // TILE
    top = layers + 1
    has_low = me_slab > 0
    has_high = me_slab < n_slab - 1
    first = me_seg == 0
    last = me_seg == n_seg - 1

    def span(c):
        return pl.ds(pl.multiple_of(c * size, size), size)

    def padded(c):
        return pl.ds(pl.multiple_of(c * size + PAD, 8), size)

    def load_u0(c):
        return pltpu.make_async_copy(
            cp.at[0, :, span(c)], u0.at[pl.ds(1, layers), padded(c)], sem_u0.at[c])

    def load_ctl(c):
        return pltpu.make_async_copy(ctl_in.at[0, :, span(c)], ctl.at[:, span(c)], sem_ctl.at[c])

    def load_rat(c):
        return pltpu.make_async_copy(rate_in.at[:, span(c)], rat.at[:, span(c)], sem_rat.at[c])

    def alt_c(c):
        return pltpu.make_async_copy(target.at[:, span(c)], cpn.at[:, span(c)], sem_alt_c.at[c])

    def alt_p(c):
        return pltpu.make_async_copy(cp.at[0, :, span(c)], prior.at[:, span(c)], sem_alt_p.at[c])

    def halo_down(k, buf, c):
        src = cp.at[0, 0, span(c)] if buf is u0 else buf.at[1, padded(c)]
        return pltpu.make_async_remote_copy(
            src, buf.at[top, padded(c)], hs.at[k, 0, c], hr.at[k, 0, c],
            device_id={"slab": me_slab - 1}, device_id_type=MESH)

    def halo_up(k, buf, c):
        src = cp.at[0, layers - 1, span(c)] if buf is u0 else buf.at[layers, padded(c)]
        return pltpu.make_async_remote_copy(
            src, buf.at[0, padded(c)], hs.at[k, 1, c], hr.at[k, 1, c],
            device_id={"slab": me_slab + 1}, device_id_type=MESH)

    def send_halo(k, buf, c):
        @pl.when(has_low)
        def _():
            halo_down(k, buf, c).start()

        @pl.when(has_high)
        def _():
            halo_up(k, buf, c).start()

    def wait_halo(k, buf, c):
        @pl.when(has_high)
        def _():
            halo_down(k, buf, c).wait_recv()

        @pl.when(has_low)
        def _():
            halo_up(k, buf, c).wait_recv()

    inner = range(1, layers - 1)
    rim = (0, layers - 1)
    parts = (pl.ds(1, layers - 2), 0, layers - 1)

    def send_cp(c, part):
        at = parts[part]
        return pltpu.make_async_remote_copy(
            cp.at[0, at, span(c)], cpn.at[at, span(c)], zs.at[part + 3, c], zr.at[part + 3, c],
            device_id={"seg": me_seg - 1}, device_id_type=MESH)

    def send_end(c, part):
        at = parts[part]
        return pltpu.make_async_remote_copy(
            end.at[at, span(c)], prior.at[at, span(c)], zs.at[part, c], zr.at[part, c],
            device_id={"seg": me_seg + 1}, device_id_type=MESH)

    barrier = pltpu.get_barrier_semaphore()
    slab_peers = [{"slab": lax.rem(me_slab + d, n_slab)} for d in range(1, n_slab)]
    seg_peers = [{"seg": lax.rem(me_seg + d, n_seg)} for d in range(1, n_seg)]
    both = [
        {"seg": lax.rem(me_seg + e, n_seg), "slab": lax.rem(me_slab + d, n_slab)}
        for e in range(1, n_seg) for d in range(1, n_slab)
    ]
    direct = n_seg * n_slab <= 32
    peers = slab_peers + seg_peers + (both if direct else [])
    for peer in peers:
        pl.semaphore_signal(barrier, inc=1, device_id=peer, device_id_type=MESH)

    @pl.loop(0, CHUNKS)
    def _(c):
        load_u0(c).start()
        load_ctl(c).start()
        load_rat(c).start()

    edge = jnp.zeros((PAD, cols), jnp.float32)
    for buf in (u0, u1, l2, l1):
        for z in range(1, top):
            buf[z, pl.ds(0, PAD), :] = edge
            buf[z, pl.ds(rows + PAD, PAD), :] = edge

    def clear(z):
        @pl.loop(0, rows // PAD)
        def _(i):
            for buf in (u0, u1, l2, l1):
                buf[z, pl.ds(pl.multiple_of(i * PAD + PAD, 8), PAD), :] = edge

    @pl.when(jnp.logical_not(has_low))
    def _():
        clear(0)

    @pl.when(jnp.logical_not(has_high))
    def _():
        clear(top)

    acc[...] = jnp.zeros_like(acc)
    pl.semaphore_wait(barrier, len(peers))

    for c in range(AHEAD):
        send_halo(0, u0, c)

    @pl.when(jnp.logical_not(first))
    def _():
        @pl.loop(0, CHUNKS)
        def _(c):
            send_cp(c, 1).start()
            send_cp(c, 2).start()

        @pl.loop(0, CHUNKS)
        def _(c):
            send_cp(c, 0).start()

    @pl.loop(0, CHUNKS)
    def _(c):
        @pl.when(last)
        def _():
            alt_c(c).start()

        @pl.when(first)
        def _():
            alt_p(c).start()

    lane = lax.broadcasted_iota(jnp.int32, (TILE, cols), 1)
    at_left = lane == 0
    at_right = lane == cols - 1

    def laplace(buf, z, r):
        tall = buf[z, pl.ds(pl.multiple_of(r - PAD, 8), TILE + 2 * PAD), :]
        mid = tall[PAD:PAD + TILE]
        beside = buf[z + 1, pl.ds(r, TILE), :] + buf[z - 1, pl.ds(r, TILE), :]
        beside = beside + (tall[PAD + 1:PAD + 1 + TILE] + tall[PAD - 1:PAD - 1 + TILE])
        right = jnp.where(at_right, 0.0, pltpu.roll(mid, cols - 1, 1))
        left = jnp.where(at_left, 0.0, pltpu.roll(mid, 1, 1))
        return mid, beside + (right + left) - 6.0 * mid

    def each_tile(c, body, zs=range(layers)):
        @pl.loop(0, tiles)
        def _(i):
            r = pl.multiple_of(c * size + i * TILE, 8)
            for z in zs:
                body(z, r, pl.ds(r, TILE), pl.multiple_of(r + PAD, 8))

    def add_square(v):
        sq = v * v
        part = sq[:PAD]
        for i in range(1, TILE // PAD):
            part = part + sq[i * PAD:(i + 1) * PAD]
        acc[...] = acc[...] + part

    def forward(src, c, dst, zs):
        def body(z, r, at, p):
            u, lap = laplace(src, z + 1, p)
            new = u + 0.1 * (lap + rat[z, at, :] * u * (1.0 - u) + ctl[z, at, :])
            if dst is u1:
                u1[z + 1, pl.ds(p, TILE), :] = new
            else:
                end[z, at, :] = new
        each_tile(c, body, zs)

    load_u0(0).wait()

    @pl.loop(0, CHUNKS + LAG_U)
    def _(i):
        @pl.when(i < CHUNKS)
        def _():
            @pl.when(i < CHUNKS - 1)
            def _():
                load_u0(i + 1).wait()
            load_ctl(i).wait()
            load_rat(i).wait()

            @pl.when(i < CHUNKS - AHEAD)
            def _():
                send_halo(0, u0, i + AHEAD)
            wait_halo(0, u0, i)
            forward(u0, i, u1, range(layers))
            send_halo(1, u1, i)

        @pl.when(jnp.logical_and(i >= 1, i <= CHUNKS))
        def _():
            c = i - 1
            forward(u1, c, end, inner)

            @pl.when(jnp.logical_not(last))
            def _():
                send_end(c, 0).start()

        @pl.when(i >= LAG_U)
        def _():
            c = i - LAG_U
            wait_halo(1, u1, c)
            forward(u1, c, end, rim)

            @pl.when(jnp.logical_not(last))
            def _():
                send_end(c, 1).start()
                send_end(c, 2).start()

    def defect(c, zs):
        def body(z, r, at, p):
            l2[z + 1, pl.ds(p, TILE), :] = end[z, at, :] - cpn[z, at, :]
        each_tile(c, body, zs)

    @pl.loop(0, CHUNKS)
    def _(c):
        @pl.when(last)
        def _():
            alt_c(c).wait()

        @pl.when(jnp.logical_not(last))
        def _():
            send_cp(c, 1).wait_recv()
            send_cp(c, 2).wait_recv()
        defect(c, rim)
        send_halo(2, l2, c)

    def do_defect(c):
        @pl.when(jnp.logical_not(last))
        def _():
            send_cp(c, 0).wait_recv()
        defect(c, inner)

    def do_l1(c):
        wait_halo(2, l2, c)

        def body(z, r, at, p):
            lam, lap = laplace(l2, z + 1, p)
            new = lam + 0.1 * (lap + rat[z, at, :] * (1.0 - 2.0 * u1[z + 1, pl.ds(p, TILE), :]) * lam)
            l1[z + 1, pl.ds(p, TILE), :] = new
            g = 0.1 * (lam + new)
            gc[z, at, :] = g
            add_square(g)
        each_tile(c, body)
        send_halo(3, l1, c)

    def do_l0(c):
        wait_halo(3, l1, c)

        def body(z, r, at, p):
            lam, lap = laplace(l1, z + 1, p)
            start = u0[z + 1, pl.ds(p, TILE), :]
            gs[z, at, :] = lam + 0.1 * (lap + rat[z, at, :] * (1.0 - 2.0 * start) * lam)
        each_tile(c, body)

    def do_start(c):
        @pl.when(first)
        def _():
            alt_p(c).wait()

        @pl.when(jnp.logical_not(first))
        def _():
            for part in range(3):
                send_end(c, part).wait_recv()

        def body(z, r, at, p):
            g = gs[z, at, :] - (prior[z, at, :] - u0[z + 1, pl.ds(p, TILE), :])
            gs[z, at, :] = g
            add_square(g)
        each_tile(c, body)

    @pl.loop(0, CHUNKS + LAG_S)
    def _(i):
        @pl.when(i < CHUNKS)
        def _():
            do_defect(i)

        @pl.when(jnp.logical_and(i >= 1, i < CHUNKS))
        def _():
            do_l1(i - 1)

        @pl.when(i == CHUNKS - 1)
        def _():
            do_l1(i)

        @pl.when(jnp.logical_and(i >= LAG_0, i < CHUNKS + LAG_0))
        def _():
            do_l0(i - LAG_0)

        @pl.when(i >= LAG_S)
        def _():
            do_start(i - LAG_S)

    tile = acc[:, :128]
    for j in range(1, cols // 128):
        tile = tile + acc[:, j * 128:(j + 1) * 128]

    def total(value, slots, owner, peers, ss, sr):
        count = len(peers)

        def copy(at, peer):
            return pltpu.make_async_remote_copy(
                slots.at[at], slots.at[at], ss, sr, device_id=peer, device_id_type=MESH)

        slots[owner] = value
        for peer in peers:
            copy(owner, peer).start()
        everything = copy(pl.ds(0, count), peers[0])
        everything.wait_recv()
        result = slots[0]
        for j in range(1, count + 1):
            result = result + slots[j]
        return result, everything

    if direct:
        tile, sent_a = total(tile, slot_a, me_seg * n_slab + me_slab, peers, as_, ar)
        sent = [sent_a]
    else:
        tile, sent_a = total(tile, slot_a, me_slab, slab_peers, as_, ar)
        tile, sent_b = total(tile, slot_b, me_seg, seg_peers, bs, br)
        sent = [sent_a, sent_b]
    tot_out[...] = tile
    for copies in sent:
        copies.wait_send()

    @pl.loop(0, CHUNKS)
    def _(c):
        for k, buf in enumerate((u0, u1, l2, l1)):
            @pl.when(has_low)
            def _():
                halo_down(k, buf, c).wait_send()

            @pl.when(has_high)
            def _():
                halo_up(k, buf, c).wait_send()

        @pl.when(jnp.logical_not(first))
        def _():
            for part in range(3):
                send_cp(c, part).wait_send()

        @pl.when(jnp.logical_not(last))
        def _():
            for part in range(3):
                send_end(c, part).wait_send()


def update_kernel(
    count, u0, ctl, gs, gc, tot, new_cp, new_ctl, out_a, out_b, sem_a, sem_b
):
    layers, rows, cols = ctl.shape
    size = rows // PARTS
    sum_of = jnp.sum(jnp.sum(tot[...], axis=0, keepdims=True), axis=1, keepdims=True)
    scale = jnp.broadcast_to(0.5 / jnp.sqrt(sum_of / count + 1e-06), (PAD, cols))

    def save(c):
        at = pl.ds(pl.multiple_of(c * size, size), size)
        return (
            pltpu.make_async_copy(out_a.at[:, at], new_cp.at[0, :, at], sem_a.at[c]),
            pltpu.make_async_copy(out_b.at[:, at], new_ctl.at[0, :, at], sem_b.at[c]),
        )

    @pl.loop(0, PARTS)
    def _(c):
        @pl.loop(0, size // PAD)
        def _(i):
            r = pl.multiple_of(c * size + i * PAD, 8)
            at = pl.ds(r, PAD)
            for z in range(layers):
                start = u0[z + 1, pl.ds(pl.multiple_of(r + PAD, 8), PAD), :]
                out_a[z, at, :] = start - scale * gs[z, at, :]
                out_b[z, at, :] = ctl[z, at, :] - scale * gc[z, at, :]
        for copy in save(c):
            copy.start()

    @pl.loop(0, PARTS)
    def _(c):
        for copy in save(c):
            copy.wait()


def per_device(checkpoints, control, rate, target):
    n_seg = lax.axis_size("seg")
    n_slab = lax.axis_size("slab")
    layers, rows, cols = rate.shape
    f32 = jnp.float32
    block = pltpu.VMEM((layers, rows, cols), f32)
    wide = pltpu.VMEM((layers + 2, rows + 2 * PAD, cols), f32)
    dma = pltpu.SemaphoreType.DMA
    hbm = pl.BlockSpec(memory_space=pltpu.HBM)
    vmem = pl.BlockSpec(memory_space=pltpu.VMEM)
    kept = pl.pallas_call(
        functools.partial(kernel, n_seg, n_slab),
        out_shape=(wide, block, block, block, pltpu.VMEM((8, 128), f32)),
        in_specs=[hbm] * 4,
        out_specs=(vmem,) * 5,
        scratch_shapes=[
            wide, wide, wide,
            block, block, block, block,
            pltpu.VMEM((PAD, cols), f32),
            pltpu.VMEM((n_slab * n_seg, 8, 128), f32),
            pltpu.VMEM((n_seg, 8, 128), f32),
            dma((CHUNKS,)), dma((CHUNKS,)), dma((CHUNKS,)),
            dma((CHUNKS,)), dma((CHUNKS,)),
            dma((4, 2, CHUNKS)), dma((4, 2, CHUNKS)),
            dma((6, CHUNKS)), dma((6, CHUNKS)),
            dma(()), dma(()), dma(()), dma(()),
        ],
        compiler_params=pltpu.CompilerParams(
            collective_id=0, has_side_effects=True, vmem_limit_bytes=50 << 20
        ),
        name="shooting",
    )(checkpoints, control, rate, target)
    count = 2.0 * n_seg * n_slab * rate.size
    return pl.pallas_call(
        functools.partial(update_kernel, count),
        out_shape=(
            jax.ShapeDtypeStruct(checkpoints.shape, f32),
            jax.ShapeDtypeStruct(control.shape, f32),
        ),
        in_specs=[vmem] * 5,
        out_specs=(hbm, hbm),
        scratch_shapes=[block, block, dma((PARTS,)), dma((PARTS,))],
        compiler_params=pltpu.CompilerParams(vmem_limit_bytes=8 << 20),
        name="update",
    )(*kept)


def solution(mesh):
    return jax.shard_map(
        per_device,
        mesh=mesh,
        in_specs=(
            P("seg", "slab", None, None),
            P("seg", "slab", None, None),
            P("slab", None, None),
            P("slab", None, None),
        ),
        out_specs=(P("seg", "slab", None, None), P("seg", "slab", None, None)),
        check_vma=False,
    )
```
